32 devices in a mesh: seq: 8 (over y, x, core), trunk: 4 (over z).
Axes of the slice: x: 2, y: 2, z: 4, core: 2. Of those that a mesh axis runs over, the one named last changes fastest.
Arguments:
- tokens: int32 [8, 131072], P('seq', 'trunk'), may hold values from 0 to 3
- first_weight: bfloat16 [128, 768], replicated, may hold values from -1 to 1
- second_weight: bfloat16 [1536, 1024], replicated, may hold values from -0.15625 to 0.15625
- third_weight: bfloat16 [2048, 1536], replicated, may hold values from -0.125 to 0.125
- norm_gain: float32 [1536], replicated, may hold values from 0.1 to 1.9
- query_weight: bfloat16 [1536, 1024], replicated, may hold values from -0.15625 to 0.15625
- context_weight: bfloat16 [1536, 320], replicated, may hold values from -0.15625 to 0.15625
- output_weight: bfloat16 [1536, 1536], replicated, may hold values from -0.15625 to 0.15625
- pair_bias: float32 [8, 8, 64, 64], P('seq', None, 'trunk'), may hold values from -6 to 300
- cotangent: bfloat16 [8, 1024, 1536], P('seq', 'trunk'), may hold values from -6 to 6
Outputs:
- encoded: bfloat16 [8, 1024, 1536], P('seq', 'trunk')
- update: bfloat16 [8, 1024, 1536], P('seq', 'trunk')
- input_gradient: bfloat16 [8, 1024, 1536], P('seq', 'trunk')
- query_gradient: float32 [1536, 1024], P(('seq', 'trunk'))
- context_gradient: float32 [1536, 320], P(('seq', 'trunk'))
- output_gradient: float32 [1536, 1536], P(('seq', 'trunk'))
The draws below stay inside these ranges and needn't reach their ends.
All inputs are finite; a program needn't handle non-finite values.
Results may differ from the reference program's by a relative error of at most 0.019.
Values may be sent and summed in bfloat16 or wider, within the bound.
A program may use at most 384 MiB of HBM per device.

```python
import math
import jax
import jax.numpy as jnp
from jax import lax

D = 1536
HEADS = 8
DK = 128
DV = 192
C1 = 768
C2 = 1024
PATCH = 32
PAIR = 16
TR = 256
SAMPLES = 8
LT = 1024
N_TRUNK = 4


def draw_pair_bias(key, part):
    blocks = TR * N_TRUNK // PAIR
    bias_shape = (SAMPLES, HEADS, blocks, blocks)
    key_base = jax.random.fold_in(key, 0)
    biases = jnp.clip(1.5 * jax.random.normal(key_base, bias_shape, jnp.float32), -6.0, 6.0)
    return biases


def touch_ends(entries, stream_key, least, high):
    longest = entries.shape.index(max(entries.shape))
    spots = []
    for shift in (0, 1):
        where = [jax.random.randint(jax.random.fold_in(stream_key, axis), (), 0, length) for axis, length in enumerate(entries.shape)]
        where[longest] = (where[longest] + shift) % entries.shape[longest]
        spots.append(tuple(where))
    return entries.at[spots[0]].set(least).at[spots[1]].set(high)


def block_levels(stream_key, shape, shards, low, high):
    level = 1.0
    for position, blocks in shards:
        steps = jax.random.uniform(jax.random.fold_in(jax.random.fold_in(stream_key, 6), position), (blocks,), jnp.float32, low / len(shards), high / len(shards))
        level = level * jnp.repeat(jnp.exp(steps), shape[position] // blocks).reshape((-1,) + (1,) * (len(shape) - 1 - position))
    return level


def normal_values(own_key, extent, spread, limit, pieces=(), kind=jnp.bfloat16):
    gain = block_levels(own_key, extent, pieces, -0.22, 0.18) if pieces else 1.0
    entries = jax.random.normal(own_key, extent, jnp.float32) * spread * gain
    return jnp.minimum(jnp.maximum(entries, -limit), limit).astype(kind)


def setup_inputs(seed: int = 0) -> dict:
    key_of = jax.random.split(jax.random.key(seed), 11)
    tokens = touch_ends(jax.random.randint(key_of[0], (SAMPLES, LT * PATCH * 4), 0, 4), jax.random.fold_in(key_of[0], 1), 0, 3).astype(jnp.int32)
    first_weight = normal_values(key_of[1], (4 * PATCH, C1), PATCH ** -0.5, 1.0)
    second_weight = normal_values(key_of[2], (2 * C1, C2), (2 * C1) ** -0.5, 0.15625)
    third_weight = normal_values(key_of[3], (2 * C2, D), (2 * C2) ** -0.5, 0.125)
    norm_gain = jnp.clip(1.0 + 0.18 * jax.random.normal(key_of[4], (D,), jnp.float32), 0.1, 1.9)
    query_weight = normal_values(key_of[5], (D, HEADS * DK), D ** -0.5, 0.15625)
    context_weight = normal_values(key_of[6], (D, DK + DV), D ** -0.5, 0.15625)
    output_weight = normal_values(key_of[7], (HEADS * DV, D), (HEADS * DV) ** -0.5, 0.15625)
    pair_bias = draw_pair_bias(jax.random.fold_in(key_of[10], 71), 0)
    cotangent = normal_values(key_of[9], (SAMPLES, LT, D), 1.0, 6.0, ((0, 8), (1, 4)))
    return {"tokens": tokens, "first_weight": first_weight, "second_weight": second_weight, "third_weight": third_weight, "norm_gain": norm_gain, "query_weight": query_weight, "context_weight": context_weight, "output_weight": output_weight, "pair_bias": pair_bias, "cotangent": cotangent}


EPS = 1e-06

def encode(tokens, first_weight, second_weight, third_weight):
    leading = tokens.shape[:-1]
    onehot = jax.nn.one_hot(tokens, 4, dtype=jnp.bfloat16)
    patches = onehot.reshape(-1, first_weight.shape[0])
    section_one = jax.nn.gelu(jnp.dot(patches, first_weight, preferred_element_type=jnp.float32)).astype(jnp.bfloat16)
    section_two = jax.nn.gelu(jnp.dot(section_one.reshape(-1, second_weight.shape[0]), second_weight, preferred_element_type=jnp.float32)).astype(jnp.bfloat16)
    encoded = jnp.dot(section_two.reshape(-1, third_weight.shape[0]), third_weight, preferred_element_type=jnp.float32).astype(jnp.bfloat16)
    row_count = tokens.shape[-1] * 4 // first_weight.shape[0] // 4
    return encoded.reshape(leading + (row_count, third_weight.shape[1]))

def add_bias(scores, biases):
    head_count, row_total, col_total = scores.shape
    blocks = scores.reshape(head_count, row_total // PAIR, PAIR, col_total // PAIR, PAIR)
    return (blocks + biases[:, :, None, :, None]).reshape(head_count, row_total, col_total)

def trunk_sample(trunk_in, norm_gain, query_weight, context_weight, output_weight, biases, cot_rows):
    inputs = trunk_in.astype(jnp.float32)
    inverse = lax.rsqrt(lax.optimization_barrier(jnp.mean(inputs * inputs, axis=-1, keepdims=True)) + EPS)
    whitened = inputs * inverse
    gains = norm_gain.astype(jnp.float32)
    normed = (whitened * gains).astype(jnp.bfloat16)
    row_total = trunk_in.shape[0]
    queries = jnp.dot(normed, query_weight, preferred_element_type=jnp.float32).astype(jnp.bfloat16)
    context = jnp.dot(normed, context_weight, preferred_element_type=jnp.float32).astype(jnp.bfloat16)
    key_rows = context[:, :DK].astype(jnp.float32)
    value_rows = context[:, DK:].astype(jnp.float32)
    score_scale = 1.0 / math.sqrt(DK)
    query_heads = queries.reshape(row_total, HEADS, DK).astype(jnp.float32)
    scores = jnp.einsum('qhd,kd->hqk', query_heads, key_rows) * score_scale
    scores = add_bias(scores, biases)
    shifted = jnp.exp(scores - lax.optimization_barrier(jnp.max(scores, axis=-1, keepdims=True)))
    soft = shifted / lax.optimization_barrier(jnp.sum(shifted, axis=-1, keepdims=True))
    soft_rounded = soft.astype(jnp.bfloat16)
    soft_wide = soft_rounded.astype(jnp.float32)
    mixture = jnp.einsum('hqk,kv->qhv', soft_wide, value_rows).reshape(row_total, HEADS * DV).astype(jnp.bfloat16)
    update = jnp.dot(mixture, output_weight, preferred_element_type=jnp.float32).astype(jnp.bfloat16)
    grad_mix = jnp.dot(cot_rows, output_weight.T, preferred_element_type=jnp.float32).astype(jnp.bfloat16)
    mix_heads = grad_mix.reshape(row_total, HEADS, DV).astype(jnp.float32)
    grad_soft = jnp.einsum('qhv,kv->hqk', mix_heads, value_rows)
    row_delta = lax.optimization_barrier(jnp.sum(soft * grad_soft, axis=-1, keepdims=True))
    grad_score = (soft * (grad_soft - row_delta)).astype(jnp.bfloat16)
    score_wide = grad_score.astype(jnp.float32)
    grad_queries = (jnp.einsum('hqk,kd->qhd', score_wide, key_rows) * score_scale).reshape(row_total, HEADS * DK).astype(jnp.bfloat16)
    grad_keys = jnp.einsum('hqk,qhd->kd', score_wide, query_heads) * score_scale
    grad_values = jnp.einsum('hqk,qhv->kv', soft_wide, mix_heads)
    grad_context = jnp.concatenate([grad_keys, grad_values], axis=-1).astype(jnp.bfloat16)
    grad_normed = jnp.dot(grad_queries, query_weight.T, preferred_element_type=jnp.float32) + jnp.dot(grad_context, context_weight.T, preferred_element_type=jnp.float32)
    grad_white = grad_normed * gains
    input_gradient = (inverse * (grad_white - whitened * lax.optimization_barrier(jnp.mean(grad_white * whitened, axis=-1, keepdims=True)))).astype(jnp.bfloat16)
    query_term = jnp.dot(normed.T, grad_queries, preferred_element_type=jnp.float32)
    context_term = jnp.dot(normed.T, grad_context, preferred_element_type=jnp.float32)
    output_term = jnp.dot(mixture.T, cot_rows, preferred_element_type=jnp.float32)
    return (update, input_gradient, query_term, context_term, output_term)

def reference(tokens, first_weight, second_weight, third_weight, norm_gain, query_weight, context_weight, output_weight, pair_bias, cotangent):
    encoded = encode(tokens, first_weight, second_weight, third_weight)

    def per_sample(totals, sample_in):
        rows_in, biases, cot_rows = sample_in
        update, input_gradient, query_term, context_term, output_term = trunk_sample(rows_in, norm_gain, query_weight, context_weight, output_weight, biases, cot_rows)
        return ((totals[0] + query_term, totals[1] + context_term, totals[2] + output_term), (update, input_gradient))
    initial = (jnp.zeros((D, HEADS * DK), jnp.float32), jnp.zeros((D, DK + DV), jnp.float32), jnp.zeros((HEADS * DV, D), jnp.float32))
    totals, outputs = lax.scan(per_sample, initial, (encoded, pair_bias, cotangent))
    factor = 1.0 / math.sqrt(SAMPLES * TR * N_TRUNK)
    return (encoded, outputs[0], outputs[1], totals[0] * factor, totals[1] * factor, totals[2] * factor)
```

```python
import math

import jax
import jax.numpy as jnp
from jax import lax
from jax.experimental import pallas as pl
from jax.experimental.pallas import tpu as pltpu
from jax.sharding import PartitionSpec as P

HEADS = 8
DK = 128
DV = 192
PAIR = 16
EPS = 1e-06
F32 = jnp.float32
BF16 = jnp.bfloat16


def encode(tokens, first_weight, second_weight, third_weight):
    taps, c1 = first_weight.shape
    patch = taps // 4
    rows = tokens.shape[-1] // (4 * patch)
    pairs = tokens.reshape(rows, 2, 2 * patch).transpose(1, 0, 2).reshape(2 * rows, 2 * patch)
    base = lax.broadcasted_iota(jnp.int32, (2 * patch, 2 * taps), 0)
    lane = lax.broadcasted_iota(jnp.int32, (2 * patch, 2 * taps), 1)
    spread = jnp.dot(
        pairs.astype(BF16), (lane // 4 == base).astype(BF16), preferred_element_type=F32
    )
    code = lax.broadcasted_iota(jnp.int32, spread.shape, 1) % 4
    onehot = (spread == code.astype(F32)).astype(BF16)
    none = jnp.zeros_like(first_weight)
    both = jnp.concatenate(
        [
            jnp.concatenate([first_weight, none], axis=1),
            jnp.concatenate([none, first_weight], axis=1),
        ],
        axis=0,
    )
    section_one = jax.nn.gelu(jnp.dot(onehot, both, preferred_element_type=F32)).astype(BF16)
    section_two = jax.nn.gelu(
        jnp.dot(section_one, second_weight, preferred_element_type=F32)
    ).astype(BF16)
    c2 = second_weight.shape[1]
    return (
        jnp.dot(section_two[:rows], third_weight[:c2], preferred_element_type=F32)
        + jnp.dot(section_two[rows:], third_weight[c2:], preferred_element_type=F32)
    ).astype(BF16)


def dot_on(a, b, da, db, **kw):
    return lax.dot_general(
        a, b, (((da,), (db,)), ((), ())), preferred_element_type=F32, **kw
    )


def attend_kernel(
    q_ref, g_ref, k_ref, v0_ref, v1_ref, b_ref, mix_ref, gq_ref, kv_ref, acck, accv
):
    step = pl.program_id(0)
    scale = 1.0 / math.sqrt(DK)
    total = k_ref.shape[0]
    rows = q_ref.shape[0]

    @pl.when(step == 0)
    def _():
        acck[...] = jnp.zeros_like(acck)
        accv[...] = jnp.zeros_like(accv)

    blocks = b_ref.shape[2]
    widen = (
        lax.shift_right_logical(
            lax.broadcasted_iota(jnp.int32, (blocks, total), 1), int(math.log2(PAIR))
        )
        == lax.broadcasted_iota(jnp.int32, (blocks, total), 0)
    ).astype(F32)
    outs = []
    for t, v_ref in enumerate((v0_ref, v1_ref)):
        q = q_ref[:, t * DK : (t + 1) * DK]
        g = g_ref[:, t * 128 : t * 128 + 256]
        bias = dot_on(b_ref[t], widen, 1, 0, precision=lax.Precision.HIGHEST)
        scores = dot_on(q, k_ref[...], 1, 1) * scale
        scores = (scores.reshape(rows // PAIR, PAIR, total) + bias[:, None, :]).reshape(rows, total)
        shifted = jnp.exp(scores - jnp.max(scores, axis=-1, keepdims=True))
        soft = shifted * (1.0 / jnp.sum(shifted, axis=-1, keepdims=True))
        rounded = soft.astype(BF16)
        outs.append(dot_on(rounded, v_ref[...], 1, 0))
        accv[:DV, :] += dot_on(g_ref[:, t * DV : (t + 1) * DV], rounded, 0, 0)
        grad_soft = dot_on(g, v_ref[...], 1, 1)
        weighted = soft * grad_soft
        delta = jnp.sum(weighted, axis=-1, keepdims=True)
        grad_score = (weighted - soft * delta).astype(BF16)
        gq_ref[:, t * DK : (t + 1) * DK] = (dot_on(grad_score, k_ref[...], 1, 0) * scale).astype(
            BF16
        )
        acck[...] += dot_on(q, grad_score, 0, 0)
    mix_ref[:, :128] = outs[0][:, :128].astype(BF16)
    mix_ref[:, 128:256] = (outs[0][:, 128:] + outs[1][:, :128]).astype(BF16)
    mix_ref[:, 256:] = outs[1][:, 128:].astype(BF16)

    @pl.when(step == pl.num_programs(0) - 1)
    def _():
        kv_ref[:, :DK] = (acck[...] * scale).T.astype(BF16)
        kv_ref[:, DK:] = accv[...].T.astype(BF16)


def attend(queries, grad_mix, key_rows, value_rows, biases):
    rows, total = queries.shape[0], key_rows.shape[0]
    first = jnp.pad(value_rows, ((0, 0), (0, 256 - DV)))
    second = jnp.pad(value_rows, ((0, 0), (256 - DV, 0)))
    whole = lambda width: pl.BlockSpec((total, width), lambda i: (0, 0))
    own = lambda width: pl.BlockSpec((rows, width), lambda i: (0, i))
    return pl.pallas_call(
        attend_kernel,
        grid=(HEADS // 2,),
        out_shape=(
            jax.ShapeDtypeStruct((rows, HEADS * DV), BF16),
            jax.ShapeDtypeStruct((rows, HEADS * DK), BF16),
            jax.ShapeDtypeStruct((total, DK + 256), BF16),
        ),
        in_specs=[
            own(2 * DK),
            own(2 * DV),
            whole(DK),
            whole(256),
            whole(256),
            pl.BlockSpec((2,) + biases.shape[1:], lambda i: (i, 0, 0)),
        ],
        out_specs=(own(2 * DV), own(2 * DK), whole(DK + 256)),
        scratch_shapes=[
            pltpu.VMEM((DK, total), F32),
            pltpu.VMEM((256, total), F32),
        ],
        cost_estimate=pl.CostEstimate(
            flops=HEADS * rows * total * 2 * (3 * DK + 3 * 256),
            bytes_accessed=4 * rows * HEADS * (DK + DV) + 4 * total * 1024,
            transcendentals=HEADS * rows * total,
        ),
        compiler_params=pltpu.CompilerParams(vmem_limit_bytes=48 * 1024 * 1024),
    )(queries, grad_mix, key_rows, first, second, biases)


def bits_of(axis):
    size = lax.axis_size(axis)
    return [1 << e for e in range(size.bit_length() - 1)]


def bit_of(axis, bit):
    return lax.axis_index(axis) // bit % 2


def swap(x, axis, bit):
    return lax.ppermute(x, axis, [(i, i ^ bit) for i in range(lax.axis_size(axis))])


def gather_trunk(x):
    rows = x.shape[0]
    x = x[None]
    for bit in reversed(bits_of("trunk")):
        other = swap(x, "trunk", bit)
        high = bit_of("trunk", bit) == 1
        x = jnp.stack([jnp.where(high, other, x), jnp.where(high, x, other)], axis=1)
        x = x.reshape((-1,) + x.shape[2:])
    return x.reshape((-1,) + x.shape[2:])


def halve(total, names, stages):
    names = list(names)
    for stage in stages:
        axis, bit = stage
        place = names.index(stage)
        names.pop(place)
        mine = bit_of(axis, bit)
        sent = lax.dynamic_index_in_dim(total, 1 - mine, place, keepdims=False).astype(BF16)
        kept = lax.dynamic_index_in_dim(total, mine, place, keepdims=False)
        got = swap(sent, axis, bit)
        total = kept.astype(F32) + got.astype(F32)
        if names:
            total = total.astype(BF16)
    return total


def scatter_product(left, right, splits):
    seq, trunk = bits_of("seq"), bits_of("trunk")
    names = [("seq", b) for b in reversed(seq[1:])] + [("trunk", b) for b in reversed(trunk)]
    own = left.shape[1] // (lax.axis_size("seq") * lax.axis_size("trunk"))
    upper = lax.axis_size("seq") // 2
    parts = left.reshape(left.shape[0], upper, 2, -1)
    mine = bit_of("seq", 1)
    pick = lambda which: lax.dynamic_index_in_dim(parts, which, 2, keepdims=False).reshape(
        left.shape[0], -1
    )
    sent = dot_on(pick(1 - mine), right, 0, 0).astype(BF16)
    got = swap(sent, "seq", 1)
    total = (dot_on(pick(mine), right, 0, 0) + got.astype(F32)).astype(BF16)
    total = total.reshape([2] * len(names) + [own, right.shape[1]])
    near = [("trunk", b) for b in trunk]
    ups = [("seq", b) for b in seq[1:]]
    done, start = [], 0
    for place, width in enumerate(splits):
        order = ups if place % 2 == 0 else ups[::-1]
        piece = lax.slice_in_dim(total, start, start + width, axis=total.ndim - 1)
        done.append(halve(piece, names, order + near))
        start += width
    return done[0] if len(done) == 1 else jnp.concatenate(done, axis=1)


def body(
    tokens,
    first_weight,
    second_weight,
    third_weight,
    norm_gain,
    query_weight,
    context_weight,
    output_weight,
    pair_bias,
    cotangent,
):
    trunk_in = encode(tokens, first_weight, second_weight, third_weight)
    row_total, width = trunk_in.shape
    inputs = trunk_in.astype(F32)
    inverse = lax.rsqrt(jnp.mean(inputs * inputs, axis=-1, keepdims=True) + EPS)
    whitened = inputs * inverse
    normed = (whitened * norm_gain).astype(BF16)
    context = jnp.dot(normed, context_weight, preferred_element_type=F32).astype(BF16)
    context_all = gather_trunk(context)
    queries = jnp.dot(normed, query_weight, preferred_element_type=F32).astype(BF16)
    cot_rows = cotangent.reshape(row_total, width)
    grad_mix = dot_on(cot_rows, output_weight, 1, 1).astype(BF16)
    mixture, grad_queries, kv_term = attend(
        queries, grad_mix, context_all[:, :DK], context_all[:, DK:], pair_bias[0]
    )
    trunk_bits = bits_of("trunk")
    kv_names = [("trunk", b) for b in reversed(trunk_bits)]
    kv_split = kv_term[:, : DK + DV].reshape([2] * len(trunk_bits) + [row_total, DK + DV])
    grad_context = halve(kv_split, kv_names, kv_names[::-1]).astype(BF16)
    update = jnp.dot(mixture, output_weight, preferred_element_type=F32).astype(BF16)
    factor = 1.0 / math.sqrt(row_total * lax.axis_size("trunk") * lax.axis_size("seq"))
    half = width // 2
    output_gradient = scatter_product(mixture, cot_rows, (half, width - half)) * factor
    cut = HEADS * DK // 2
    query_gradient = scatter_product(normed, grad_queries, (cut, cut)) * factor
    grad_normed = dot_on(grad_queries, query_weight, 1, 1) + dot_on(
        grad_context, context_weight, 1, 1
    )
    grad_white = grad_normed * norm_gain
    input_gradient = (
        inverse * (grad_white - whitened * jnp.mean(grad_white * whitened, axis=-1, keepdims=True))
    ).astype(BF16)
    context_gradient = scatter_product(normed, grad_context, (DK + DV,)) * factor
    return (
        trunk_in.reshape(1, row_total, width),
        update.reshape(1, row_total, width),
        input_gradient.reshape(1, row_total, width),
        query_gradient,
        context_gradient,
        output_gradient,
    )


def solution(mesh):
    placed = (
        P("seq", "trunk"),
        P(),
        P(),
        P(),
        P(),
        P(),
        P(),
        P(),
        P("seq", None, "trunk", None),
        P("seq", "trunk", None),
    )
    return jax.shard_map(
        body,
        mesh=mesh,
        in_specs=placed,
        out_specs=(
            P("seq", "trunk", None),
            P("seq", "trunk", None),
            P("seq", "trunk", None),
            P(("seq", "trunk"), None),
            P(("seq", "trunk"), None),
            P(("seq", "trunk"), None),
        ),
        check_vma=False,
    )
```

```python
import math

import jax
import jax.numpy as jnp
from jax import lax
from jax.experimental import pallas as pl
from jax.experimental.pallas import tpu as pltpu
from jax.sharding import PartitionSpec as P

HEADS = 8
DK = 128
DV = 192
PAIR = 16
EPS = 1e-06
F32 = jnp.float32
BF16 = jnp.bfloat16


def encode(tokens, first_weight, second_weight, third_weight):
    taps, c1 = first_weight.shape
    patch = taps // 4
    rows = tokens.shape[-1] // (4 * patch)
    pairs = tokens.reshape(rows, 2, 2 * patch).transpose(1, 0, 2).reshape(2 * rows, 2 * patch)
    base = lax.broadcasted_iota(jnp.int32, (2 * patch, 2 * taps), 0)
    lane = lax.broadcasted_iota(jnp.int32, (2 * patch, 2 * taps), 1)
    spread = jnp.dot(
        pairs.astype(BF16), (lane // 4 == base).astype(BF16), preferred_element_type=F32
    )
    code = lax.broadcasted_iota(jnp.int32, spread.shape, 1) % 4
    onehot = (spread == code.astype(F32)).astype(BF16)
    none = jnp.zeros_like(first_weight)
    both = jnp.concatenate(
        [
            jnp.concatenate([first_weight, none], axis=1),
            jnp.concatenate([none, first_weight], axis=1),
        ],
        axis=0,
    )
    section_one = jax.nn.gelu(jnp.dot(onehot, both, preferred_element_type=F32)).astype(BF16)
    section_two = jax.nn.gelu(
        jnp.dot(section_one, second_weight, preferred_element_type=F32)
    ).astype(BF16)
    c2 = second_weight.shape[1]
    return (
        jnp.dot(section_two[:rows], third_weight[:c2], preferred_element_type=F32)
        + jnp.dot(section_two[rows:], third_weight[c2:], preferred_element_type=F32)
    ).astype(BF16)


def dot_on(a, b, da, db, **kw):
    return lax.dot_general(
        a, b, (((da,), (db,)), ((), ())), preferred_element_type=F32, **kw
    )


def attend_kernel(
    q_ref, g_ref, k_ref, v0_ref, v1_ref, b_ref, mix_ref, gq_ref, kv_ref, acck, accv
):
    step = pl.program_id(0)
    scale = 1.0 / math.sqrt(DK)
    total = k_ref.shape[0]
    rows = q_ref.shape[0]

    @pl.when(step == 0)
    def _():
        acck[...] = jnp.zeros_like(acck)
        accv[...] = jnp.zeros_like(accv)

    blocks = b_ref.shape[2]
    widen = (
        lax.shift_right_logical(
            lax.broadcasted_iota(jnp.int32, (blocks, total), 1), int(math.log2(PAIR))
        )
        == lax.broadcasted_iota(jnp.int32, (blocks, total), 0)
    ).astype(F32)
    outs = []
    for t, v_ref in enumerate((v0_ref, v1_ref)):
        q = q_ref[:, t * DK : (t + 1) * DK]
        g = g_ref[:, t * 128 : t * 128 + 256]
        bias = dot_on(b_ref[t], widen, 1, 0, precision=lax.Precision.HIGHEST)
        scores = dot_on(q, k_ref[...], 1, 1) * scale
        scores = (scores.reshape(rows // PAIR, PAIR, total) + bias[:, None, :]).reshape(rows, total)
        shifted = jnp.exp(scores - jnp.max(scores, axis=-1, keepdims=True))
        soft = shifted * (1.0 / jnp.sum(shifted, axis=-1, keepdims=True))
        rounded = soft.astype(BF16)
        outs.append(dot_on(rounded, v_ref[...], 1, 0))
        accv[:DV, :] += dot_on(g_ref[:, t * DV : (t + 1) * DV], rounded, 0, 0)
        grad_soft = dot_on(g, v_ref[...], 1, 1)
        weighted = soft * grad_soft
        delta = jnp.sum(weighted, axis=-1, keepdims=True)
        grad_score = (weighted - soft * delta).astype(BF16)
        gq_ref[:, t * DK : (t + 1) * DK] = (dot_on(grad_score, k_ref[...], 1, 0) * scale).astype(
            BF16
        )
        acck[...] += dot_on(q, grad_score, 0, 0)
    mix_ref[:, :128] = outs[0][:, :128].astype(BF16)
    mix_ref[:, 128:256] = (outs[0][:, 128:] + outs[1][:, :128]).astype(BF16)
    mix_ref[:, 256:] = outs[1][:, 128:].astype(BF16)

    @pl.when(step == pl.num_programs(0) - 1)
    def _():
        kv_ref[:, :DK] = (acck[...] * scale).T.astype(BF16)
        kv_ref[:, DK:] = accv[...].T.astype(BF16)


def attend(queries, grad_mix, key_rows, value_rows, biases):
    rows, total = queries.shape[0], key_rows.shape[0]
    first = jnp.pad(value_rows, ((0, 0), (0, 256 - DV)))
    second = jnp.pad(value_rows, ((0, 0), (256 - DV, 0)))
    whole = lambda width: pl.BlockSpec((total, width), lambda i: (0, 0))
    own = lambda width: pl.BlockSpec((rows, width), lambda i: (0, i))
    return pl.pallas_call(
        attend_kernel,
        grid=(HEADS // 2,),
        out_shape=(
            jax.ShapeDtypeStruct((rows, HEADS * DV), BF16),
            jax.ShapeDtypeStruct((rows, HEADS * DK), BF16),
            jax.ShapeDtypeStruct((total, DK + 256), BF16),
        ),
        in_specs=[
            own(2 * DK),
            own(2 * DV),
            whole(DK),
            whole(256),
            whole(256),
            pl.BlockSpec((2,) + biases.shape[1:], lambda i: (i, 0, 0)),
        ],
        out_specs=(own(2 * DV), own(2 * DK), whole(DK + 256)),
        scratch_shapes=[
            pltpu.VMEM((DK, total), F32),
            pltpu.VMEM((256, total), F32),
        ],
        cost_estimate=pl.CostEstimate(
            flops=HEADS * rows * total * 2 * (3 * DK + 3 * 256),
            bytes_accessed=4 * rows * HEADS * (DK + DV) + 4 * total * 1024,
            transcendentals=HEADS * rows * total,
        ),
        compiler_params=pltpu.CompilerParams(vmem_limit_bytes=48 * 1024 * 1024),
    )(queries, grad_mix, key_rows, first, second, biases)


def bits_of(axis):
    size = lax.axis_size(axis)
    return [1 << e for e in range(size.bit_length() - 1)]


def bit_of(axis, bit):
    return lax.axis_index(axis) // bit % 2


def swap(x, axis, bit):
    return lax.ppermute(x, axis, [(i, i ^ bit) for i in range(lax.axis_size(axis))])


def gather_trunk(x):
    rows = x.shape[0]
    x = x[None]
    for bit in reversed(bits_of("trunk")):
        other = swap(x, "trunk", bit)
        high = bit_of("trunk", bit) == 1
        x = jnp.stack([jnp.where(high, other, x), jnp.where(high, x, other)], axis=1)
        x = x.reshape((-1,) + x.shape[2:])
    return x.reshape((-1,) + x.shape[2:])


def halve(total, names, stages):
    names = list(names)
    for stage in stages:
        axis, bit = stage
        place = names.index(stage)
        names.pop(place)
        mine = bit_of(axis, bit)
        sent = lax.dynamic_index_in_dim(total, 1 - mine, place, keepdims=False).astype(BF16)
        kept = lax.dynamic_index_in_dim(total, mine, place, keepdims=False)
        got = swap(sent, axis, bit)
        total = kept.astype(F32) + got.astype(F32)
        if names:
            total = total.astype(BF16)
    return total


def near_product(left, right):
    upper = lax.axis_size("seq") // 2
    parts = left.reshape(left.shape[0], upper, 2, -1)
    mine = bit_of("seq", 1)
    pick = lambda which: lax.dynamic_index_in_dim(parts, which, 2, keepdims=False).reshape(
        left.shape[0], -1
    )
    sent = dot_on(pick(1 - mine), right, 0, 0).astype(BF16)
    got = swap(sent, "seq", 1)
    return (dot_on(pick(mine), right, 0, 0) + got.astype(F32)).astype(BF16)


def scatter_rows(pieces):
    seq, trunk = bits_of("seq"), bits_of("trunk")
    names = [("seq", b) for b in reversed(seq[1:])] + [("trunk", b) for b in reversed(trunk)]
    near = [("trunk", b) for b in trunk]
    ups = [("seq", b) for b in seq[1:]]
    return [
        halve(piece.reshape([2] * len(names) + [-1, piece.shape[1]]), names, order + near)
        for piece, order in zip(pieces, (ups, ups[::-1]))
    ]


def body(
    tokens,
    first_weight,
    second_weight,
    third_weight,
    norm_gain,
    query_weight,
    context_weight,
    output_weight,
    pair_bias,
    cotangent,
):
    trunk_in = encode(tokens, first_weight, second_weight, third_weight)
    row_total, width = trunk_in.shape
    inputs = trunk_in.astype(F32)
    inverse = lax.rsqrt(jnp.mean(inputs * inputs, axis=-1, keepdims=True) + EPS)
    whitened = inputs * inverse
    normed = (whitened * norm_gain).astype(BF16)
    context = jnp.dot(normed, context_weight, preferred_element_type=F32).astype(BF16)
    context_all = gather_trunk(context)
    queries = jnp.dot(normed, query_weight, preferred_element_type=F32).astype(BF16)
    cot_rows = cotangent.reshape(row_total, width)
    grad_mix = dot_on(cot_rows, output_weight, 1, 1).astype(BF16)
    mixture, grad_queries, kv_term = attend(
        queries, grad_mix, context_all[:, :DK], context_all[:, DK:], pair_bias[0]
    )
    trunk_bits = bits_of("trunk")
    kv_names = [("trunk", b) for b in reversed(trunk_bits)]
    kv_split = kv_term[:, : DK + DV].reshape([2] * len(trunk_bits) + [row_total, DK + DV])
    grad_context = halve(kv_split, kv_names, kv_names[::-1]).astype(BF16)
    update = jnp.dot(mixture, output_weight, preferred_element_type=F32).astype(BF16)
    factor = 1.0 / math.sqrt(row_total * lax.axis_size("trunk") * lax.axis_size("seq"))
    output_near = near_product(mixture, cot_rows)
    query_near = near_product(normed, grad_queries)
    grad_normed = dot_on(grad_queries, query_weight, 1, 1) + dot_on(
        grad_context, context_weight, 1, 1
    )
    grad_white = grad_normed * norm_gain
    input_gradient = (
        inverse * (grad_white - whitened * jnp.mean(grad_white * whitened, axis=-1, keepdims=True))
    ).astype(BF16)
    context_near = near_product(normed, grad_context)
    cut = (width + HEADS * DK + DK + DV) // 256 * 128
    first, second = scatter_rows(
        (
            output_near[:, :cut],
            jnp.concatenate([output_near[:, cut:], query_near, context_near], axis=1),
        )
    )
    rest = width - cut
    output_gradient = jnp.concatenate([first, second[:, :rest]], axis=1) * factor
    query_gradient = second[:, rest : rest + HEADS * DK] * factor
    context_gradient = second[:, rest + HEADS * DK :] * factor
    return (
        trunk_in.reshape(1, row_total, width),
        update.reshape(1, row_total, width),
        input_gradient.reshape(1, row_total, width),
        query_gradient,
        context_gradient,
        output_gradient,
    )


def solution(mesh):
    placed = (
        P("seq", "trunk"),
        P(),
        P(),
        P(),
        P(),
        P(),
        P(),
        P(),
        P("seq", None, "trunk", None),
        P("seq", "trunk", None),
    )
    return jax.shard_map(
        body,
        mesh=mesh,
        in_specs=placed,
        out_specs=(
            P("seq", "trunk", None),
            P("seq", "trunk", None),
            P("seq", "trunk", None),
            P(("seq", "trunk"), None),
            P(("seq", "trunk"), None),
            P(("seq", "trunk"), None),
        ),
        check_vma=False,
    )
```
